256 devices in a mesh: sky: 32 (over z_lo, y, core), edge: 8 (over x, z_hi).
Axes of the slice: x: 4, y: 4, z: 8 (z_hi: 2, z_lo: 4; z = z_hi * 4 + z_lo), core: 2. Of those that a mesh axis runs over, the one named last changes fastest.
Arguments:
- node_feats: bfloat16 [131072, 128], P('sky'), may hold values from -6 to 6
- saved_agg: bfloat16 [131072, 128], P('sky'), may hold values from -9 to 9
- node_cot: bfloat16 [131072, 128], P('sky'), may hold values from -6 to 6
- edge_feats: bfloat16 [2097152, 128], P(('sky', 'edge')), may hold values from -6 to 6
- edge_cot: bfloat16 [2097152, 128], P(('sky', 'edge')), may hold values from -6 to 6
- senders: int32 [2097152], P(('sky', 'edge')), may hold values from 0 to 8191, as said below
- counts: int32 [131072], P('sky'), may hold values from 0 to 16, as said below
- send_lower: int32 [65536], P('sky'), may hold values from 0 to 4095, as said below
- send_upper: int32 [65536], P('sky'), may hold values from 0 to 4095, as said below
- w_recv: bfloat16 [128, 128], replicated, may hold values from -0.3125 to 0.3125
- w_send: bfloat16 [128, 128], replicated, may hold values from -0.3125 to 0.3125
- w_edge: bfloat16 [128, 128], replicated, may hold values from -0.3125 to 0.3125
- w_out: bfloat16 [128, 128], replicated, may hold values from -0.5 to 0.5
- b_edge: float32 [128], replicated, may hold values from -3 to 3
- v_self: bfloat16 [128, 128], replicated, may hold values from -0.375 to 0.375
- v_agg: bfloat16 [128, 128], replicated, may hold values from -0.375 to 0.375
- v_out: bfloat16 [128, 128], replicated, may hold values from -0.5 to 0.5
- b_node: float32 [128], replicated, may hold values from -3 to 3
Outputs:
- node_grad: bfloat16 [131072, 128], P('sky')
- edge_grad: bfloat16 [2097152, 128], P(('sky', 'edge'))
- edge_weight_grads: float32 [4, 128, 128], replicated
- node_weight_grads: float32 [3, 128, 128], replicated
- bias_grads: float32 [2, 128], replicated
The draws below stay inside these ranges and needn't reach their ends.
Inputs may be any that keep to these rules, and one draw needn't show every extreme that they name: `senders`: A sender below 4096 is a node of the receiver's own tile; from 4096 up it is a halo slot of halo_rows. Dead slots name a sender too. `counts`: counts differ from tile to tile. `send_lower`: each tile's 2048 entries are distinct node rows of that tile. `send_upper`: each tile's 2048 entries are distinct node rows of that tile.
All inputs are finite; a program needn't handle non-finite values.
Results may differ from the reference program's by a relative error of at most 0.012.
Values may be sent and summed in bfloat16 or wider, within the bound.
A program may use at most 128 MiB of HBM per device.

```python
import jax
import jax.numpy as jnp
from jax import lax

FEAT = 128
DEGREE = 16
TILE_NODES = 4096
HALO = 2048
TILES = 32
NODES = 131072
EDGES = 2097152


def draw_senders(key, part):
    key = jax.random.fold_in(key, 3)
    first, second, third = jax.random.split(key, 3)
    local = jax.random.randint(first, (EDGES,), 0, TILE_NODES)
    remote = jax.random.randint(second, (EDGES,), TILE_NODES, TILE_NODES + 2 * HALO)
    picker = jax.random.randint(third, (EDGES,), 0, 4)
    result = jnp.where(picker < 3, local, remote)
    result = result.at[0].set(0).at[1].set(TILE_NODES + 2 * HALO - 1)
    return result.astype(jnp.int32)


def draw_counts(key, part):
    key = jax.random.fold_in(key, 4)
    first, second, third, fourth = jax.random.split(key, 4)
    ceiling = jax.random.randint(first, (TILES,), 6, DEGREE + 1)
    ceiling = ceiling.at[jax.random.randint(second, (), 0, TILES)].set(DEGREE)
    result = jax.random.randint(third, (TILES, TILE_NODES), ceiling[:, None] // 2, ceiling[:, None] + 1)
    where_top = jax.random.randint(fourth, (TILES,), 0, TILE_NODES)
    tile_rows = jnp.arange(TILES)
    result = result.at[tile_rows, where_top].set(ceiling)
    result = result.at[tile_rows, (where_top + 1) % TILE_NODES].set(0)
    return result.reshape(NODES).astype(jnp.int32)


def send_list(key):

    def one_tile(tile_key):
        first, second = jax.random.split(tile_key)
        middle = jax.random.permutation(first, TILE_NODES - 2) + 1
        listed = jnp.concatenate([jnp.array([0, TILE_NODES - 1], dtype=jnp.int32), middle[:HALO - 2].astype(jnp.int32)])
        order = jax.random.permutation(second, HALO)
        return listed[order]
    keys = jax.random.split(key, TILES)
    return jax.vmap(one_tile)(keys).reshape(TILES * HALO).astype(jnp.int32)


def draw_send_lower(key, part):
    return send_list(jax.random.fold_in(key, 1))


def draw_send_upper(key, part):
    return send_list(jax.random.fold_in(key, 2))


def level_of(own_key, dims, cuts, low, largest):
    level = 1.0
    for axis_at, blocks in cuts:
        draws = jax.random.uniform(jax.random.fold_in(jax.random.fold_in(own_key, 6), axis_at), (blocks,), jnp.float32, low / len(cuts), largest / len(cuts))
        level = level * jnp.repeat(jnp.exp(draws), dims[axis_at] // blocks).reshape((-1,) + (1,) * (len(dims) - 1 - axis_at))
    return level


def gaussian(rng, dims, deviation, bound, shards=(), kind=jnp.bfloat16):
    factor_of = level_of(rng, dims, shards, -0.22, 0.18) if shards else 1.0
    values = jax.random.normal(rng, dims, jnp.float32) * deviation * factor_of
    return jnp.minimum(jnp.maximum(values, -bound), bound).astype(kind)


def setup_inputs(seed: int = 0) -> dict:
    key_of = jax.random.split(jax.random.key(seed), 19)
    return {
        "node_feats": gaussian(key_of[0], (NODES, FEAT), 1.0, 6.0, ((0, 32),)),
        "saved_agg": gaussian(key_of[1], (NODES, FEAT), 1.5, 9.0, ((0, 32),)),
        "node_cot": gaussian(key_of[2], (NODES, FEAT), 1.0, 6.0, ((0, 32),)),
        "edge_feats": gaussian(key_of[3], (EDGES, FEAT), 1.0, 6.0, ((0, 256),)),
        "edge_cot": gaussian(key_of[4], (EDGES, FEAT), 1.0, 6.0, ((0, 256),)),
        "senders": draw_senders(jax.random.fold_in(key_of[18], 71), 0),
        "counts": draw_counts(jax.random.fold_in(key_of[18], 71), 0),
        "send_lower": draw_send_lower(jax.random.fold_in(key_of[18], 71), 0),
        "send_upper": draw_send_upper(jax.random.fold_in(key_of[18], 71), 0),
        "w_recv": gaussian(key_of[9], (FEAT, FEAT), (3 * FEAT) ** -0.5, 0.3125),
        "w_send": gaussian(key_of[10], (FEAT, FEAT), (3 * FEAT) ** -0.5, 0.3125),
        "w_edge": gaussian(key_of[11], (FEAT, FEAT), (3 * FEAT) ** -0.5, 0.3125),
        "w_out": gaussian(key_of[12], (FEAT, FEAT), FEAT ** -0.5, 0.5),
        "b_edge": gaussian(key_of[13], (FEAT,), 0.7, 3.0, (), jnp.float32),
        "v_self": gaussian(key_of[14], (FEAT, FEAT), (2 * FEAT) ** -0.5, 0.375),
        "v_agg": gaussian(key_of[15], (FEAT, FEAT), (2 * FEAT) ** -0.5, 0.375),
        "v_out": gaussian(key_of[16], (FEAT, FEAT), FEAT ** -0.5, 0.5),
        "b_node": gaussian(key_of[17], (FEAT,), 0.7, 3.0, (), jnp.float32),
    }


def slope(z):
    s = jax.nn.sigmoid(z)
    return s * (1.0 + z * (1.0 - s))

def mm(a, b):
    return jnp.dot(a, b, preferred_element_type=jnp.float32)

def outer_sum(a, b):
    return jnp.einsum('ef,eg->fg', a.astype(jnp.float32), b.astype(jnp.float32))

def reference(node_feats, saved_agg, node_cot, edge_feats, edge_cot, senders, counts, send_lower, send_upper, w_recv, w_send, w_edge, w_out, b_edge, v_self, v_agg, v_out, b_node):
    tiles = node_feats.reshape(TILES, TILE_NODES, FEAT)
    lower_list = send_lower.reshape(TILES, HALO)
    upper_list = send_upper.reshape(TILES, HALO)
    upper_rows = jax.vmap(lambda a, i: jnp.take(a, i, axis=0))(tiles, upper_list)
    lower_rows = jax.vmap(lambda a, i: jnp.take(a, i, axis=0))(tiles, lower_list)
    from_lower = jnp.roll(upper_rows, 1, axis=0)
    from_upper = jnp.roll(lower_rows, -1, axis=0)

    def one_tile(args):
        feats, agg, cot, efeat, ecot, send, cnt, low, high = args
        all_rows = jnp.concatenate([feats, low, high], axis=0)
        sender_rows = jnp.take(all_rows, send, axis=0)
        pre_edge = jnp.repeat(mm(feats, w_recv), DEGREE, axis=0) + mm(sender_rows, w_send) + mm(efeat, w_edge) + b_edge
        hidden = jax.nn.silu(pre_edge).astype(jnp.bfloat16)
        pre_node = mm(feats, v_self) + mm(agg, v_agg) + b_node
        node_act = jax.nn.silu(pre_node).astype(jnp.bfloat16)
        d_pre_node = (mm(cot, v_out.T) * slope(pre_node)).astype(jnp.bfloat16)
        d_agg = mm(d_pre_node, v_agg.T).astype(jnp.bfloat16)
        d_node = cot.astype(jnp.float32) + mm(d_pre_node, v_self.T)
        live = (jnp.arange(DEGREE, dtype=jnp.int32)[None, :] < cnt[:, None]).astype(jnp.float32).reshape(-1, 1)
        d_msg = ((ecot.astype(jnp.float32) + jnp.repeat(d_agg.astype(jnp.float32), DEGREE, axis=0)) * live).astype(jnp.bfloat16)
        d_pre = (mm(d_msg, w_out.T) * slope(pre_edge)).astype(jnp.bfloat16)
        egrad = mm(d_pre, w_edge.T).astype(jnp.bfloat16)
        to_recv = mm(d_pre, w_recv.T).reshape(TILE_NODES, DEGREE, FEAT).sum(axis=1)
        to_send = jax.ops.segment_sum(mm(d_pre, w_send.T), send, num_segments=TILE_NODES + 2 * HALO)
        local = to_send[:TILE_NODES] + d_node + to_recv
        recv_rows = jnp.repeat(feats, DEGREE, axis=0)
        ewg = jnp.stack([outer_sum(recv_rows, d_pre), outer_sum(sender_rows, d_pre), outer_sum(efeat, d_pre), outer_sum(hidden, d_msg)])
        nwg = jnp.stack([outer_sum(feats, d_pre_node), outer_sum(agg, d_pre_node), outer_sum(node_act, cot)])
        bg = jnp.stack([lax.optimization_barrier(jnp.sum(d_pre.astype(jnp.float32), axis=0)), lax.optimization_barrier(jnp.sum(d_pre_node.astype(jnp.float32), axis=0))])
        return (local, to_send[TILE_NODES:TILE_NODES + HALO], to_send[TILE_NODES + HALO:], egrad, ewg, nwg, bg)
    xs = (tiles, saved_agg.reshape(TILES, TILE_NODES, FEAT), node_cot.reshape(TILES, TILE_NODES, FEAT), edge_feats.reshape(TILES, TILE_NODES * DEGREE, FEAT), edge_cot.reshape(TILES, TILE_NODES * DEGREE, FEAT), senders.reshape(TILES, TILE_NODES * DEGREE), counts.reshape(TILES, TILE_NODES), from_lower, from_upper)
    local, cot_lower, cot_upper, egrad, ewg, nwg, bg = lax.map(one_tile, xs)
    back_upper = jnp.roll(cot_lower, -1, axis=0)
    back_lower = jnp.roll(cot_upper, 1, axis=0)
    local = jax.vmap(lambda z, i, c: z.at[i].add(c))(local, upper_list, back_upper)
    local = jax.vmap(lambda z, i, c: z.at[i].add(c))(local, lower_list, back_lower)
    scale = 1.0 / jnp.sqrt(jnp.float32(EDGES))
    node_grad = local.reshape(NODES, FEAT).astype(jnp.bfloat16)
    return (node_grad, egrad.reshape(EDGES, FEAT), lax.optimization_barrier(jnp.sum(ewg, axis=0)) * scale, lax.optimization_barrier(jnp.sum(nwg, axis=0)) * scale, lax.optimization_barrier(jnp.sum(bg, axis=0)) * scale)
```

```python
import jax
import jax.numpy as jnp
from jax import lax
from jax.sharding import PartitionSpec as P

DEGREE = 16


def passed_along(array, axis, by):
    size = lax.axis_size(axis)
    return lax.ppermute(array, axis, [(i, (i + by) % size) for i in range(size)])


def slope(z):
    s = jax.nn.sigmoid(z)
    return s * (1.0 + z * (1.0 - s))


def matmul(a, b):
    return jnp.dot(a, b, preferred_element_type=jnp.float32)


def outer_sum(a, b):
    return jnp.einsum("ef,eg->fg", a, b, preferred_element_type=jnp.float32)


def shards(
    node_feats,
    saved_agg,
    node_cot,
    edge_feats,
    edge_cot,
    senders,
    counts,
    send_lower,
    send_upper,
    w_recv,
    w_send,
    w_edge,
    w_out,
    b_edge,
    v_self,
    v_agg,
    v_out,
    b_node,
):
    nodes = node_feats.shape[0]
    width = node_feats.shape[1]
    halo = send_lower.shape[0]
    groups = lax.axis_size("edge")
    member = lax.axis_index("edge")
    share = nodes // groups
    start = member * share
    upper_rows = jnp.take(node_feats, send_upper, axis=0)
    lower_rows = jnp.take(node_feats, send_lower, axis=0)
    from_lower = passed_along(upper_rows, "sky", 1)
    from_upper = passed_along(lower_rows, "sky", -1)
    all_rows = jnp.concatenate([node_feats, from_lower, from_upper], axis=0)
    own = lax.dynamic_slice_in_dim(node_feats, start, share, 0)
    own_agg = lax.dynamic_slice_in_dim(saved_agg, start, share, 0)
    own_cot = lax.dynamic_slice_in_dim(node_cot, start, share, 0)
    own_counts = lax.dynamic_slice_in_dim(counts, start, share, 0)
    pre_node = matmul(own, v_self) + matmul(own_agg, v_agg) + b_node
    node_act = jax.nn.silu(pre_node).astype(jnp.bfloat16)
    d_pre_node = (matmul(own_cot, v_out.T) * slope(pre_node)).astype(jnp.bfloat16)
    d_agg = matmul(d_pre_node, v_agg.T).astype(jnp.bfloat16)
    d_node = own_cot.astype(jnp.float32) + matmul(d_pre_node, v_self.T)
    sender_rows = jnp.take(all_rows, senders, axis=0)
    pre_edge = (
        jnp.repeat(matmul(own, w_recv), DEGREE, axis=0)
        + matmul(sender_rows, w_send)
        + matmul(edge_feats, w_edge)
        + b_edge
    )
    hidden = jax.nn.silu(pre_edge).astype(jnp.bfloat16)
    live = (
        (jnp.arange(DEGREE, dtype=jnp.int32)[None, :] < own_counts[:, None])
        .astype(jnp.float32)
        .reshape(-1, 1)
    )
    d_msg = (
        (edge_cot.astype(jnp.float32) + jnp.repeat(d_agg.astype(jnp.float32), DEGREE, axis=0))
        * live
    ).astype(jnp.bfloat16)
    d_pre = (matmul(d_msg, w_out.T) * slope(pre_edge)).astype(jnp.bfloat16)
    edge_grad = matmul(d_pre, w_edge.T).astype(jnp.bfloat16)
    to_recv = matmul(d_pre, w_recv.T).reshape(share, DEGREE, width).sum(axis=1)
    to_send = jax.ops.segment_sum(matmul(d_pre, w_send.T), senders, num_segments=nodes + 2 * halo)
    local = to_send[:nodes]
    cot_lower = to_send[nodes : nodes + halo]
    cot_upper = to_send[nodes + halo :]
    back_upper = passed_along(cot_lower.astype(jnp.bfloat16), "sky", -1).astype(cot_lower.dtype)
    back_lower = passed_along(cot_upper.astype(jnp.bfloat16), "sky", 1).astype(cot_upper.dtype)
    local = local.at[send_upper].add(back_upper).at[send_lower].add(back_lower)
    recv_grad = jnp.einsum(
        "nf,nkg->fg", own, d_pre.reshape(share, DEGREE, width), preferred_element_type=jnp.float32
    )
    bias_terms = jnp.stack(
        [
            jnp.sum(d_pre.astype(jnp.float32), axis=0),
            jnp.sum(d_pre_node.astype(jnp.float32), axis=0),
        ]
    )
    terms = jnp.concatenate(
        [
            recv_grad,
            outer_sum(sender_rows, d_pre),
            outer_sum(edge_feats, d_pre),
            outer_sum(hidden, d_msg),
            outer_sum(own, d_pre_node),
            outer_sum(own_agg, d_pre_node),
            outer_sum(node_act, own_cot),
            bias_terms,
        ],
        axis=0,
    )
    used = terms.shape[0]
    chunk = -(-used // (groups * 8)) * 8
    terms = jnp.pad(terms, ((0, chunk * groups - used), (0, 0)))
    terms = lax.psum(terms, "sky")
    mine = lax.dynamic_slice_in_dim(local, start, share, 0) + d_node + to_recv
    local = lax.dynamic_update_slice_in_dim(local, mine, start, 0)
    summed = lax.psum(jnp.concatenate([local, terms], axis=0), "edge")
    node_grad = summed[:nodes].astype(jnp.bfloat16)
    totals = summed[nodes : nodes + used]
    scale = 1.0 / jnp.sqrt(jnp.float32(lax.axis_size("sky") * nodes * DEGREE))
    totals = totals * scale
    blocks = width
    edge_total = totals[: 4 * blocks].reshape(4, blocks, width)
    node_total = totals[4 * blocks : 7 * blocks].reshape(3, blocks, width)
    bias_total = totals[7 * blocks :]
    return (node_grad, edge_grad, edge_total, node_total, bias_total)


def solution(mesh):
    in_specs = (
        P("sky", None),
        P("sky", None),
        P("sky", None),
        P(("sky", "edge"), None),
        P(("sky", "edge"), None),
        P(("sky", "edge")),
        P("sky"),
        P("sky"),
        P("sky"),
        P(),
        P(),
        P(),
        P(),
        P(),
        P(),
        P(),
        P(),
        P(),
    )
    out_specs = (P("sky", None), P(("sky", "edge"), None), P(), P(), P())
    return jax.shard_map(shards, mesh=mesh, in_specs=in_specs, out_specs=out_specs, check_vma=False)
```

```python
import jax
import jax.numpy as jnp
from jax import lax
from jax.sharding import PartitionSpec as P

DEGREE = 16


def passed_along(array, axis, by):
    size = lax.axis_size(axis)
    return lax.ppermute(array, axis, [(i, (i + by) % size) for i in range(size)])


EDGE_ORDER = (1, 2, 0)


def exchanged(array, axis, bit):
    size = lax.axis_size(axis)
    return lax.ppermute(array, axis, [(i, i ^ (1 << bit)) for i in range(size)])


def halving_sum(blocks, axis, me, order):
    bits = len(order)
    rest = blocks.shape[1:]
    x = blocks.reshape((2,) * bits + rest)
    axes = list(range(bits - 1, -1, -1))
    for bit in order:
        at = axes.index(bit)
        keep = (me >> bit) & 1
        mine = lax.dynamic_index_in_dim(x, keep, axis=at, keepdims=False)
        other = lax.dynamic_index_in_dim(x, 1 - keep, axis=at, keepdims=False)
        x = mine + exchanged(other, axis, bit)
        axes.pop(at)
    return x


def doubling_gather(block, axis, me, order):
    axes = []
    for bit in reversed(order):
        got = exchanged(block, axis, bit)
        low = ((me >> bit) & 1) == 0
        block = jnp.where(low, jnp.stack([block, got]), jnp.stack([got, block]))
        axes.insert(0, bit)
    bits = len(order)
    block = jnp.transpose(block, [axes.index(b) for b in range(bits - 1, -1, -1)] + list(range(bits, block.ndim)))
    return block.reshape((-1,) + block.shape[bits + 1 :])


def slope(z):
    s = jax.nn.sigmoid(z)
    return s * (1.0 + z * (1.0 - s))


def matmul(a, b):
    return jnp.dot(a, b, preferred_element_type=jnp.float32)


def outer_sum(a, b):
    return jnp.einsum("ef,eg->fg", a, b, preferred_element_type=jnp.float32)


def shards(
    node_feats,
    saved_agg,
    node_cot,
    edge_feats,
    edge_cot,
    senders,
    counts,
    send_lower,
    send_upper,
    w_recv,
    w_send,
    w_edge,
    w_out,
    b_edge,
    v_self,
    v_agg,
    v_out,
    b_node,
):
    nodes = node_feats.shape[0]
    width = node_feats.shape[1]
    halo = send_lower.shape[0]
    groups = lax.axis_size("edge")
    member = lax.axis_index("edge")
    share = nodes // groups
    start = member * share
    upper_rows = jnp.take(node_feats, send_upper, axis=0)
    lower_rows = jnp.take(node_feats, send_lower, axis=0)
    from_lower = passed_along(upper_rows, "sky", 1)
    from_upper = passed_along(lower_rows, "sky", -1)
    all_rows = jnp.concatenate([node_feats, from_lower, from_upper], axis=0)
    own = lax.dynamic_slice_in_dim(node_feats, start, share, 0)
    own_agg = lax.dynamic_slice_in_dim(saved_agg, start, share, 0)
    own_cot = lax.dynamic_slice_in_dim(node_cot, start, share, 0)
    own_counts = lax.dynamic_slice_in_dim(counts, start, share, 0)
    pre_node = matmul(own, v_self) + matmul(own_agg, v_agg) + b_node
    node_act = jax.nn.silu(pre_node).astype(jnp.bfloat16)
    d_pre_node = (matmul(own_cot, v_out.T) * slope(pre_node)).astype(jnp.bfloat16)
    d_agg = matmul(d_pre_node, v_agg.T).astype(jnp.bfloat16)
    d_node = own_cot.astype(jnp.float32) + matmul(d_pre_node, v_self.T)
    sender_rows = jnp.take(all_rows, senders, axis=0)
    pre_edge = (
        jnp.repeat(matmul(own, w_recv), DEGREE, axis=0)
        + matmul(sender_rows, w_send)
        + matmul(edge_feats, w_edge)
        + b_edge
    )
    hidden = jax.nn.silu(pre_edge).astype(jnp.bfloat16)
    live = (
        (jnp.arange(DEGREE, dtype=jnp.int32)[None, :] < own_counts[:, None])
        .astype(jnp.float32)
        .reshape(-1, 1)
    )
    d_msg = (
        (edge_cot.astype(jnp.float32) + jnp.repeat(d_agg.astype(jnp.float32), DEGREE, axis=0))
        * live
    ).astype(jnp.bfloat16)
    d_pre = (matmul(d_msg, w_out.T) * slope(pre_edge)).astype(jnp.bfloat16)
    edge_grad = matmul(d_pre, w_edge.T).astype(jnp.bfloat16)
    to_recv = matmul(d_pre, w_recv.T).reshape(share, DEGREE, width).sum(axis=1)
    to_send = jax.ops.segment_sum(matmul(d_pre, w_send.T), senders, num_segments=nodes + 2 * halo)
    local = to_send[:nodes]
    cot_lower = to_send[nodes : nodes + halo]
    cot_upper = to_send[nodes + halo :]
    back_upper = passed_along(cot_lower.astype(jnp.bfloat16), "sky", -1).astype(cot_lower.dtype)
    back_lower = passed_along(cot_upper.astype(jnp.bfloat16), "sky", 1).astype(cot_upper.dtype)
    local = local.at[send_upper].add(back_upper).at[send_lower].add(back_lower)
    recv_grad = jnp.einsum(
        "nf,nkg->fg", own, d_pre.reshape(share, DEGREE, width), preferred_element_type=jnp.float32
    )
    bias_terms = jnp.stack(
        [
            jnp.sum(d_pre.astype(jnp.float32), axis=0),
            jnp.sum(d_pre_node.astype(jnp.float32), axis=0),
        ]
    )
    terms = jnp.concatenate(
        [
            recv_grad,
            outer_sum(sender_rows, d_pre),
            outer_sum(edge_feats, d_pre),
            outer_sum(hidden, d_msg),
            outer_sum(own, d_pre_node),
            outer_sum(own_agg, d_pre_node),
            outer_sum(node_act, own_cot),
            bias_terms,
        ],
        axis=0,
    )
    used = terms.shape[0]
    chunk = -(-used // (groups * 8)) * 8
    terms = jnp.pad(terms, ((0, chunk * groups - used), (0, 0)))
    mine = lax.dynamic_slice_in_dim(local, start, share, 0) + d_node + to_recv
    local = lax.dynamic_update_slice_in_dim(local, mine, start, 0)
    packed = jnp.concatenate(
        [local.reshape(groups, share, width), terms.reshape(groups, chunk, width)], axis=1
    )
    summed = halving_sum(packed, "edge", member, EDGE_ORDER)
    node_grad = doubling_gather(summed[:share].astype(jnp.bfloat16), "edge", member, EDGE_ORDER)
    totals = summed[share:]
    for bit in range(lax.axis_size("sky").bit_length() - 1):
        totals = totals + exchanged(totals, "sky", bit)
    totals = doubling_gather(totals, "edge", member, EDGE_ORDER)[:used]
    scale = 1.0 / jnp.sqrt(jnp.float32(lax.axis_size("sky") * nodes * DEGREE))
    totals = totals * scale
    blocks = width
    edge_total = totals[: 4 * blocks].reshape(4, blocks, width)
    node_total = totals[4 * blocks : 7 * blocks].reshape(3, blocks, width)
    bias_total = totals[7 * blocks :]
    return (node_grad, edge_grad, edge_total, node_total, bias_total)


def solution(mesh):
    in_specs = (
        P("sky", None),
        P("sky", None),
        P("sky", None),
        P(("sky", "edge"), None),
        P(("sky", "edge"), None),
        P(("sky", "edge")),
        P("sky"),
        P("sky"),
        P("sky"),
        P(),
        P(),
        P(),
        P(),
        P(),
        P(),
        P(),
        P(),
        P(),
    )
    out_specs = (P("sky", None), P(("sky", "edge"), None), P(), P(), P())
    return jax.shard_map(shards, mesh=mesh, in_specs=in_specs, out_specs=out_specs, check_vma=False)
```

```python
import jax
import jax.numpy as jnp
from jax import lax
from jax.sharding import PartitionSpec as P


DEGREE = 16


def passed_along(array, axis, by):
    size = lax.axis_size(axis)
    return lax.ppermute(array, axis, [(i, (i + by) % size) for i in range(size)])


EDGE_ORDER = (1, 2, 0)


def exchanged(array, axis, bit):
    size = lax.axis_size(axis)
    return lax.ppermute(array, axis, [(i, i ^ (1 << bit)) for i in range(size)])


def halving_sum(blocks, axis, me, order):
    bits = len(order)
    rest = blocks.shape[1:]
    x = blocks.reshape((2,) * bits + rest)
    axes = list(range(bits - 1, -1, -1))
    for bit in order:
        at = axes.index(bit)
        keep = (me >> bit) & 1
        mine = lax.dynamic_index_in_dim(x, keep, axis=at, keepdims=False)
        other = lax.dynamic_index_in_dim(x, 1 - keep, axis=at, keepdims=False)
        x = mine + exchanged(other, axis, bit)
        axes.pop(at)
    return x


def doubling_gather(block, axis, me, order):
    axes = []
    for bit in reversed(order):
        got = exchanged(block, axis, bit)
        low = ((me >> bit) & 1) == 0
        block = jnp.where(low, jnp.stack([block, got]), jnp.stack([got, block]))
        axes.insert(0, bit)
    bits = len(order)
    block = jnp.transpose(block, [axes.index(b) for b in range(bits - 1, -1, -1)] + list(range(bits, block.ndim)))
    return block.reshape((-1,) + block.shape[bits + 1 :])


def slope(z):
    s = jax.nn.sigmoid(z)
    return s * (1.0 + z * (1.0 - s))


def matmul(a, b):
    return jnp.dot(a, b, preferred_element_type=jnp.float32)


def outer_sum(a, b):
    return jnp.einsum("ef,eg->fg", a, b, preferred_element_type=jnp.float32)


def layer(
    node_feats,
    saved_agg,
    node_cot,
    edge_feats,
    edge_cot,
    senders,
    counts,
    send_lower,
    send_upper,
    w_recv,
    w_send,
    w_edge,
    w_out,
    b_edge,
    v_self,
    v_agg,
    v_out,
    b_node,
):
    nodes = node_feats.shape[0]
    width = node_feats.shape[1]
    halo = send_lower.shape[0]
    groups = lax.axis_size("edge")
    member = lax.axis_index("edge")
    share = nodes // groups
    start = member * share
    upper_rows = node_feats.at[send_upper].get(mode="promise_in_bounds", unique_indices=True)
    lower_rows = node_feats.at[send_lower].get(mode="promise_in_bounds", unique_indices=True)
    from_lower = passed_along(upper_rows, "sky", 1)
    from_upper = passed_along(lower_rows, "sky", -1)
    all_rows = jnp.concatenate([node_feats, from_lower, from_upper], axis=0)
    own = lax.dynamic_slice_in_dim(node_feats, start, share, 0)
    own_agg = lax.dynamic_slice_in_dim(saved_agg, start, share, 0)
    own_cot = lax.dynamic_slice_in_dim(node_cot, start, share, 0)
    own_counts = lax.dynamic_slice_in_dim(counts, start, share, 0)
    pre_node = matmul(own, v_self) + matmul(own_agg, v_agg) + b_node
    node_act = jax.nn.silu(pre_node).astype(jnp.bfloat16)
    d_pre_node = (matmul(own_cot, v_out.T) * slope(pre_node)).astype(jnp.bfloat16)
    d_agg = matmul(d_pre_node, v_agg.T).astype(jnp.bfloat16)
    d_node = own_cot.astype(jnp.float32) + matmul(d_pre_node, v_self.T)
    sender_rows = all_rows.at[senders].get(mode="promise_in_bounds")
    pre_edge = (
        jnp.repeat(matmul(own, w_recv), DEGREE, axis=0)
        + matmul(sender_rows, w_send)
        + matmul(edge_feats, w_edge)
        + b_edge
    )
    hidden = jax.nn.silu(pre_edge).astype(jnp.bfloat16)
    live = (
        (jnp.arange(DEGREE, dtype=jnp.int32)[None, :] < own_counts[:, None])
        .astype(jnp.float32)
        .reshape(-1, 1)
    )
    d_msg = (
        (edge_cot.astype(jnp.float32) + jnp.repeat(d_agg.astype(jnp.float32), DEGREE, axis=0))
        * live
    ).astype(jnp.bfloat16)
    d_pre = (matmul(d_msg, w_out.T) * slope(pre_edge)).astype(jnp.bfloat16)
    edge_grad = matmul(d_pre, w_edge.T).astype(jnp.bfloat16)
    to_recv = matmul(d_pre, w_recv.T).reshape(share, DEGREE, width).sum(axis=1)
    to_send = jax.ops.segment_sum(matmul(d_pre, w_send.T), senders, num_segments=nodes + 2 * halo, mode="promise_in_bounds"
    )
    local = to_send[:nodes]
    cot_lower = to_send[nodes : nodes + halo]
    cot_upper = to_send[nodes + halo :]
    back_upper = passed_along(cot_lower.astype(jnp.bfloat16), "sky", -1).astype(cot_lower.dtype)
    back_lower = passed_along(cot_upper.astype(jnp.bfloat16), "sky", 1).astype(cot_upper.dtype)
    local = local.at[send_upper].add(back_upper, mode="promise_in_bounds", unique_indices=True)
    local = local.at[send_lower].add(back_lower, mode="promise_in_bounds", unique_indices=True)
    recv_grad = jnp.einsum(
        "nf,nkg->fg", own, d_pre.reshape(share, DEGREE, width), preferred_element_type=jnp.float32
    )
    bias_terms = jnp.stack(
        [
            jnp.sum(d_pre.astype(jnp.float32), axis=0),
            jnp.sum(d_pre_node.astype(jnp.float32), axis=0),
        ]
    )
    terms = jnp.concatenate(
        [
            recv_grad,
            outer_sum(sender_rows, d_pre),
            outer_sum(edge_feats, d_pre),
            outer_sum(hidden, d_msg),
            outer_sum(own, d_pre_node),
            outer_sum(own_agg, d_pre_node),
            outer_sum(node_act, own_cot),
            bias_terms,
        ],
        axis=0,
    )
    rounds = [("sky", bit) for bit in range(lax.axis_size("sky").bit_length() - 1)]
    rounds += [("edge", bit) for bit in EDGE_ORDER]
    for axis, bit in rounds:
        got = exchanged(terms, axis, bit)
        terms = terms + got
    mine = lax.dynamic_slice_in_dim(local, start, share, 0) + d_node + to_recv
    local = lax.dynamic_update_slice_in_dim(local, mine, start, 0)
    summed = halving_sum(local.reshape(groups, share, width), "edge", member, EDGE_ORDER)
    node_grad = doubling_gather(summed.astype(jnp.bfloat16), "edge", member, EDGE_ORDER)
    totals = terms
    scale = 1.0 / jnp.sqrt(jnp.float32(lax.axis_size("sky") * nodes * DEGREE))
    totals = totals * scale
    blocks = width
    edge_total = totals[: 4 * blocks].reshape(4, blocks, width)
    node_total = totals[4 * blocks : 7 * blocks].reshape(3, blocks, width)
    bias_total = totals[7 * blocks :]
    return (node_grad, edge_grad, edge_total, node_total, bias_total)


def solution(mesh):
    in_specs = (
        P("sky", None),
        P("sky", None),
        P("sky", None),
        P(("sky", "edge"), None),
        P(("sky", "edge"), None),
        P(("sky", "edge")),
        P("sky"),
        P("sky"),
        P("sky"),
        P(),
        P(),
        P(),
        P(),
        P(),
        P(),
        P(),
        P(),
        P(),
    )
    out_specs = (P("sky", None), P(("sky", "edge"), None), P(), P(), P())
    return jax.shard_map(layer, mesh=mesh, in_specs=in_specs, out_specs=out_specs, check_vma=False)
```

```python
import jax
import jax.numpy as jnp
from jax import lax
from jax.sharding import PartitionSpec as P


DEGREE = 16


def passed_along(array, axis, by):
    size = lax.axis_size(axis)
    return lax.ppermute(array, axis, [(i, (i + by) % size) for i in range(size)])


EDGE_ORDER = (1, 2, 0)
EARLY_ROUNDS = 3


def exchanged(array, axis, bit):
    size = lax.axis_size(axis)
    return lax.ppermute(array, axis, [(i, i ^ (1 << bit)) for i in range(size)])


def halving_sum(blocks, axis, me, order):
    bits = len(order)
    rest = blocks.shape[1:]
    x = blocks.reshape((2,) * bits + rest)
    axes = list(range(bits - 1, -1, -1))
    for bit in order:
        at = axes.index(bit)
        keep = (me >> bit) & 1
        mine = lax.dynamic_index_in_dim(x, keep, axis=at, keepdims=False)
        other = lax.dynamic_index_in_dim(x, 1 - keep, axis=at, keepdims=False)
        x = mine + exchanged(other, axis, bit)
        axes.pop(at)
    return x


def doubling_gather(block, axis, me, order):
    axes = []
    for bit in reversed(order):
        got = exchanged(block, axis, bit)
        low = ((me >> bit) & 1) == 0
        block = jnp.where(low, jnp.stack([block, got]), jnp.stack([got, block]))
        axes.insert(0, bit)
    bits = len(order)
    block = jnp.transpose(block, [axes.index(b) for b in range(bits - 1, -1, -1)] + list(range(bits, block.ndim)))
    return block.reshape((-1,) + block.shape[bits + 1 :])


def slope(z):
    s = jax.nn.sigmoid(z)
    return s * (1.0 + z * (1.0 - s))


def matmul(a, b):
    return jnp.dot(a, b, preferred_element_type=jnp.float32)


def outer_sum(a, b):
    return jnp.einsum("ef,eg->fg", a, b, preferred_element_type=jnp.float32)


def layer(
    node_feats,
    saved_agg,
    node_cot,
    edge_feats,
    edge_cot,
    senders,
    counts,
    send_lower,
    send_upper,
    w_recv,
    w_send,
    w_edge,
    w_out,
    b_edge,
    v_self,
    v_agg,
    v_out,
    b_node,
):
    nodes = node_feats.shape[0]
    width = node_feats.shape[1]
    halo = send_lower.shape[0]
    groups = lax.axis_size("edge")
    member = lax.axis_index("edge")
    share = nodes // groups
    start = member * share
    upper_rows = node_feats.at[send_upper].get(mode="promise_in_bounds", unique_indices=True)
    lower_rows = node_feats.at[send_lower].get(mode="promise_in_bounds", unique_indices=True)
    from_lower = passed_along(upper_rows, "sky", 1)
    from_upper = passed_along(lower_rows, "sky", -1)
    all_rows = jnp.concatenate([node_feats, from_lower, from_upper], axis=0)
    own = lax.dynamic_slice_in_dim(node_feats, start, share, 0)
    own_agg = lax.dynamic_slice_in_dim(saved_agg, start, share, 0)
    own_cot = lax.dynamic_slice_in_dim(node_cot, start, share, 0)
    own_counts = lax.dynamic_slice_in_dim(counts, start, share, 0)
    pre_node = matmul(own, v_self) + matmul(own_agg, v_agg) + b_node
    node_act = jax.nn.silu(pre_node).astype(jnp.bfloat16)
    d_pre_node = (matmul(own_cot, v_out.T) * slope(pre_node)).astype(jnp.bfloat16)
    d_agg = matmul(d_pre_node, v_agg.T).astype(jnp.bfloat16)
    d_node = own_cot.astype(jnp.float32) + matmul(d_pre_node, v_self.T)
    sender_rows = all_rows.at[senders].get(mode="promise_in_bounds")
    pre_edge = (
        jnp.repeat(matmul(own, w_recv), DEGREE, axis=0)
        + matmul(sender_rows, w_send)
        + matmul(edge_feats, w_edge)
        + b_edge
    )
    hidden = jax.nn.silu(pre_edge).astype(jnp.bfloat16)
    live = (
        (jnp.arange(DEGREE, dtype=jnp.int32)[None, :] < own_counts[:, None])
        .astype(jnp.float32)
        .reshape(-1, 1)
    )
    d_msg = (
        (edge_cot.astype(jnp.float32) + jnp.repeat(d_agg.astype(jnp.float32), DEGREE, axis=0))
        * live
    ).astype(jnp.bfloat16)
    d_pre = (matmul(d_msg, w_out.T) * slope(pre_edge)).astype(jnp.bfloat16)
    edge_grad = matmul(d_pre, w_edge.T).astype(jnp.bfloat16)
    to_recv = matmul(d_pre, w_recv.T).reshape(share, DEGREE, width).sum(axis=1)
    to_send = jax.ops.segment_sum(matmul(d_pre, w_send.T), senders, num_segments=nodes + 2 * halo, mode="promise_in_bounds"
    )
    local = to_send[:nodes]
    cot_lower = to_send[nodes : nodes + halo]
    cot_upper = to_send[nodes + halo :]
    back_upper = passed_along(cot_lower.astype(jnp.bfloat16), "sky", -1).astype(cot_lower.dtype)
    back_lower = passed_along(cot_upper.astype(jnp.bfloat16), "sky", 1).astype(cot_upper.dtype)
    local = local.at[send_upper].add(back_upper, mode="promise_in_bounds", unique_indices=True)
    local = local.at[send_lower].add(back_lower, mode="promise_in_bounds", unique_indices=True)
    recv_grad = jnp.einsum(
        "nf,nkg->fg", own, d_pre.reshape(share, DEGREE, width), preferred_element_type=jnp.float32
    )
    bias_terms = jnp.stack(
        [
            jnp.sum(d_pre.astype(jnp.float32), axis=0),
            jnp.sum(d_pre_node.astype(jnp.float32), axis=0),
        ]
    )
    terms = jnp.concatenate(
        [
            recv_grad,
            outer_sum(sender_rows, d_pre),
            outer_sum(edge_feats, d_pre),
            outer_sum(hidden, d_msg),
            outer_sum(own, d_pre_node),
            outer_sum(own_agg, d_pre_node),
            outer_sum(node_act, own_cot),
            bias_terms,
        ],
        axis=0,
    )
    used = terms.shape[0]
    chunk = -(-used // (groups * 8)) * 8
    terms = jnp.pad(terms, ((0, chunk * groups - used), (0, 0)))
    sky_bits = lax.axis_size("sky").bit_length() - 1
    early = min(EARLY_ROUNDS, sky_bits)
    for bit in range(early):
        got = exchanged(terms, "sky", bit)
        terms = terms + got
    mine = lax.dynamic_slice_in_dim(local, start, share, 0) + d_node + to_recv
    local = lax.dynamic_update_slice_in_dim(local, mine, start, 0)
    packed = jnp.concatenate(
        [local.reshape(groups, share, width), terms.reshape(groups, chunk, width)], axis=1
    )
    summed = halving_sum(packed, "edge", member, EDGE_ORDER)
    node_grad = doubling_gather(summed[:share].astype(jnp.bfloat16), "edge", member, EDGE_ORDER)
    totals = summed[share:]
    for bit in range(early, sky_bits):
        totals = totals + exchanged(totals, "sky", bit)
    totals = doubling_gather(totals, "edge", member, EDGE_ORDER)[:used]
    scale = 1.0 / jnp.sqrt(jnp.float32(lax.axis_size("sky") * nodes * DEGREE))
    totals = totals * scale
    blocks = width
    edge_total = totals[: 4 * blocks].reshape(4, blocks, width)
    node_total = totals[4 * blocks : 7 * blocks].reshape(3, blocks, width)
    bias_total = totals[7 * blocks :]
    return (node_grad, edge_grad, edge_total, node_total, bias_total)


def solution(mesh):
    in_specs = (
        P("sky", None),
        P("sky", None),
        P("sky", None),
        P(("sky", "edge"), None),
        P(("sky", "edge"), None),
        P(("sky", "edge")),
        P("sky"),
        P("sky"),
        P("sky"),
        P(),
        P(),
        P(),
        P(),
        P(),
        P(),
        P(),
        P(),
        P(),
    )
    out_specs = (P("sky", None), P(("sky", "edge"), None), P(), P(), P())
    return jax.shard_map(layer, mesh=mesh, in_specs=in_specs, out_specs=out_specs, check_vma=False)
```

```python
import jax
import jax.numpy as jnp
from jax import lax
from jax.sharding import PartitionSpec as P


DEGREE = 16


def passed_along(array, axis, by):
    size = lax.axis_size(axis)
    return lax.ppermute(array, axis, [(i, (i + by) % size) for i in range(size)])


EDGE_ORDER = (1, 2, 0)
EARLY_ROUNDS = 3


def exchanged(array, axis, bit):
    size = lax.axis_size(axis)
    return lax.ppermute(array, axis, [(i, i ^ (1 << bit)) for i in range(size)])


def halving_sum(blocks, axis, me, order):
    bits = len(order)
    rest = blocks.shape[1:]
    x = blocks.reshape((2,) * bits + rest)
    axes = list(range(bits - 1, -1, -1))
    for bit in order:
        at = axes.index(bit)
        keep = (me >> bit) & 1
        mine = lax.dynamic_index_in_dim(x, keep, axis=at, keepdims=False)
        other = lax.dynamic_index_in_dim(x, 1 - keep, axis=at, keepdims=False)
        x = mine + exchanged(other, axis, bit)
        axes.pop(at)
    return x


def doubling_gather(block, axis, me, order):
    axes = []
    for bit in reversed(order):
        got = exchanged(block, axis, bit)
        low = ((me >> bit) & 1) == 0
        block = jnp.where(low, jnp.stack([block, got]), jnp.stack([got, block]))
        axes.insert(0, bit)
    bits = len(order)
    block = jnp.transpose(block, [axes.index(b) for b in range(bits - 1, -1, -1)] + list(range(bits, block.ndim)))
    return block.reshape((-1,) + block.shape[bits + 1 :])


def picker(rows, size):
    return (rows[:, None] == lax.broadcasted_iota(jnp.int32, (1, size), 1)).astype(jnp.bfloat16)


def spread(pick, values):
    return lax.dot_general(
        pick, values, (((0,), (0,)), ((), ())), preferred_element_type=jnp.float32
    )


def slope(z):
    s = jax.nn.sigmoid(z)
    return s * (1.0 + z * (1.0 - s))


def matmul(a, b):
    return jnp.dot(a, b, preferred_element_type=jnp.float32)


def outer_sum(a, b):
    return jnp.einsum("ef,eg->fg", a, b, preferred_element_type=jnp.float32)


def layer(
    node_feats,
    saved_agg,
    node_cot,
    edge_feats,
    edge_cot,
    senders,
    counts,
    send_lower,
    send_upper,
    w_recv,
    w_send,
    w_edge,
    w_out,
    b_edge,
    v_self,
    v_agg,
    v_out,
    b_node,
):
    nodes = node_feats.shape[0]
    width = node_feats.shape[1]
    halo = send_lower.shape[0]
    groups = lax.axis_size("edge")
    member = lax.axis_index("edge")
    share = nodes // groups
    start = member * share
    upper_pick = picker(send_upper, nodes)
    lower_pick = picker(send_lower, nodes)
    upper_rows = matmul(upper_pick, node_feats).astype(jnp.bfloat16)
    lower_rows = matmul(lower_pick, node_feats).astype(jnp.bfloat16)
    from_lower = passed_along(upper_rows, "sky", 1)
    from_upper = passed_along(lower_rows, "sky", -1)
    all_rows = jnp.concatenate([node_feats, from_lower, from_upper], axis=0)
    own = lax.dynamic_slice_in_dim(node_feats, start, share, 0)
    own_agg = lax.dynamic_slice_in_dim(saved_agg, start, share, 0)
    own_cot = lax.dynamic_slice_in_dim(node_cot, start, share, 0)
    own_counts = lax.dynamic_slice_in_dim(counts, start, share, 0)
    pre_node = matmul(own, v_self) + matmul(own_agg, v_agg) + b_node
    node_act = jax.nn.silu(pre_node).astype(jnp.bfloat16)
    d_pre_node = (matmul(own_cot, v_out.T) * slope(pre_node)).astype(jnp.bfloat16)
    d_agg = matmul(d_pre_node, v_agg.T).astype(jnp.bfloat16)
    d_node = own_cot.astype(jnp.float32) + matmul(d_pre_node, v_self.T)
    sender_rows = all_rows.at[senders].get(mode="promise_in_bounds")
    pre_edge = (
        jnp.repeat(matmul(own, w_recv), DEGREE, axis=0)
        + matmul(sender_rows, w_send)
        + matmul(edge_feats, w_edge)
        + b_edge
    )
    hidden = jax.nn.silu(pre_edge).astype(jnp.bfloat16)
    live = (
        (jnp.arange(DEGREE, dtype=jnp.int32)[None, :] < own_counts[:, None])
        .astype(jnp.float32)
        .reshape(-1, 1)
    )
    d_msg = (
        (edge_cot.astype(jnp.float32) + jnp.repeat(d_agg.astype(jnp.float32), DEGREE, axis=0))
        * live
    ).astype(jnp.bfloat16)
    d_pre = (matmul(d_msg, w_out.T) * slope(pre_edge)).astype(jnp.bfloat16)
    edge_grad = matmul(d_pre, w_edge.T).astype(jnp.bfloat16)
    to_recv = matmul(d_pre, w_recv.T).reshape(share, DEGREE, width).sum(axis=1)
    to_send = jax.ops.segment_sum(matmul(d_pre, w_send.T), senders, num_segments=nodes + 2 * halo, mode="promise_in_bounds"
    )
    local = to_send[:nodes]
    cot_lower = to_send[nodes : nodes + halo]
    cot_upper = to_send[nodes + halo :]
    back_upper = passed_along(cot_lower.astype(jnp.bfloat16), "sky", -1)
    back_lower = passed_along(cot_upper.astype(jnp.bfloat16), "sky", 1)
    local = local + spread(upper_pick, back_upper)
    local = local + spread(lower_pick, back_lower)
    recv_grad = jnp.einsum(
        "nf,nkg->fg", own, d_pre.reshape(share, DEGREE, width), preferred_element_type=jnp.float32
    )
    bias_terms = jnp.stack(
        [
            jnp.sum(d_pre.astype(jnp.float32), axis=0),
            jnp.sum(d_pre_node.astype(jnp.float32), axis=0),
        ]
    )
    terms = jnp.concatenate(
        [
            recv_grad,
            outer_sum(sender_rows, d_pre),
            outer_sum(edge_feats, d_pre),
            outer_sum(hidden, d_msg),
            outer_sum(own, d_pre_node),
            outer_sum(own_agg, d_pre_node),
            outer_sum(node_act, own_cot),
            bias_terms,
        ],
        axis=0,
    )
    used = terms.shape[0]
    chunk = -(-used // (groups * 8)) * 8
    terms = jnp.pad(terms, ((0, chunk * groups - used), (0, 0)))
    sky_bits = lax.axis_size("sky").bit_length() - 1
    early = min(EARLY_ROUNDS, sky_bits)
    for bit in range(early):
        got = exchanged(terms, "sky", bit)
        terms = terms + got
    mine = lax.dynamic_slice_in_dim(local, start, share, 0) + d_node + to_recv
    local = lax.dynamic_update_slice_in_dim(local, mine, start, 0)
    packed = jnp.concatenate(
        [local.reshape(groups, share, width), terms.reshape(groups, chunk, width)], axis=1
    )
    summed = halving_sum(packed, "edge", member, EDGE_ORDER)
    node_grad = doubling_gather(summed[:share].astype(jnp.bfloat16), "edge", member, EDGE_ORDER)
    totals = summed[share:]
    for bit in range(early, sky_bits):
        totals = totals + exchanged(totals, "sky", bit)
    totals = doubling_gather(totals, "edge", member, EDGE_ORDER)[:used]
    scale = 1.0 / jnp.sqrt(jnp.float32(lax.axis_size("sky") * nodes * DEGREE))
    totals = totals * scale
    blocks = width
    edge_total = totals[: 4 * blocks].reshape(4, blocks, width)
    node_total = totals[4 * blocks : 7 * blocks].reshape(3, blocks, width)
    bias_total = totals[7 * blocks :]
    return (node_grad, edge_grad, edge_total, node_total, bias_total)


def solution(mesh):
    in_specs = (
        P("sky", None),
        P("sky", None),
        P("sky", None),
        P(("sky", "edge"), None),
        P(("sky", "edge"), None),
        P(("sky", "edge")),
        P("sky"),
        P("sky"),
        P("sky"),
        P(),
        P(),
        P(),
        P(),
        P(),
        P(),
        P(),
        P(),
        P(),
    )
    out_specs = (P("sky", None), P(("sky", "edge"), None), P(), P(), P())
    return jax.shard_map(layer, mesh=mesh, in_specs=in_specs, out_specs=out_specs, check_vma=False)
```

```python
import jax
import jax.numpy as jnp
from jax import lax
from jax.sharding import PartitionSpec as P


DEGREE = 16


def passed_along(array, axis, by):
    size = lax.axis_size(axis)
    return lax.ppermute(array, axis, [(i, (i + by) % size) for i in range(size)])


EDGE_ORDER = (1, 2, 0)
EARLY_ROUNDS = 3


def exchanged(array, axis, bit):
    size = lax.axis_size(axis)
    return lax.ppermute(array, axis, [(i, i ^ (1 << bit)) for i in range(size)])


def halving_sum(blocks, axis, me, order, wire=None):
    bits = len(order)
    rest = blocks.shape[1:]
    x = blocks.reshape((2,) * bits + rest)
    axes = list(range(bits - 1, -1, -1))
    for bit in order:
        at = axes.index(bit)
        keep = (me >> bit) & 1
        mine = lax.dynamic_index_in_dim(x, keep, axis=at, keepdims=False)
        other = lax.dynamic_index_in_dim(x, 1 - keep, axis=at, keepdims=False)
        if wire is None:
            x = mine + exchanged(other, axis, bit)
        else:
            x = mine + exchanged(other.astype(wire), axis, bit).astype(mine.dtype)
        axes.pop(at)
    return x


def doubling_gather(block, axis, me, order):
    axes = []
    for bit in reversed(order):
        got = exchanged(block, axis, bit)
        low = ((me >> bit) & 1) == 0
        block = jnp.where(low, jnp.stack([block, got]), jnp.stack([got, block]))
        axes.insert(0, bit)
    bits = len(order)
    block = jnp.transpose(block, [axes.index(b) for b in range(bits - 1, -1, -1)] + list(range(bits, block.ndim)))
    return block.reshape((-1,) + block.shape[bits + 1 :])


def picker(rows, size):
    return (rows[:, None] == lax.broadcasted_iota(jnp.int32, (1, size), 1)).astype(jnp.bfloat16)


def spread(pick, values):
    return lax.dot_general(
        pick, values, (((0,), (0,)), ((), ())), preferred_element_type=jnp.float32
    )


def slope(z):
    s = jax.nn.sigmoid(z)
    return s * (1.0 + z * (1.0 - s))


def matmul(a, b):
    return jnp.dot(a, b, preferred_element_type=jnp.float32)


def outer_sum(a, b):
    return jnp.einsum("ef,eg->fg", a, b, preferred_element_type=jnp.float32)


def layer(
    node_feats,
    saved_agg,
    node_cot,
    edge_feats,
    edge_cot,
    senders,
    counts,
    send_lower,
    send_upper,
    w_recv,
    w_send,
    w_edge,
    w_out,
    b_edge,
    v_self,
    v_agg,
    v_out,
    b_node,
):
    nodes = node_feats.shape[0]
    width = node_feats.shape[1]
    halo = send_lower.shape[0]
    groups = lax.axis_size("edge")
    member = lax.axis_index("edge")
    share = nodes // groups
    start = member * share
    upper_pick = picker(send_upper, nodes)
    lower_pick = picker(send_lower, nodes)
    upper_rows = matmul(upper_pick, node_feats).astype(jnp.bfloat16)
    lower_rows = matmul(lower_pick, node_feats).astype(jnp.bfloat16)
    from_lower = passed_along(upper_rows, "sky", 1)
    from_upper = passed_along(lower_rows, "sky", -1)
    all_rows = jnp.concatenate([node_feats, from_lower, from_upper], axis=0)
    own = lax.dynamic_slice_in_dim(node_feats, start, share, 0)
    own_agg = lax.dynamic_slice_in_dim(saved_agg, start, share, 0)
    own_cot = lax.dynamic_slice_in_dim(node_cot, start, share, 0)
    own_counts = lax.dynamic_slice_in_dim(counts, start, share, 0)
    pre_node = matmul(own, v_self) + matmul(own_agg, v_agg) + b_node
    node_act = jax.nn.silu(pre_node).astype(jnp.bfloat16)
    d_pre_node = (matmul(own_cot, v_out.T) * slope(pre_node)).astype(jnp.bfloat16)
    d_agg = matmul(d_pre_node, v_agg.T).astype(jnp.bfloat16)
    d_node = own_cot.astype(jnp.float32) + matmul(d_pre_node, v_self.T)
    sender_rows = all_rows.at[senders].get(mode="promise_in_bounds")
    pre_edge = (
        jnp.repeat(matmul(own, w_recv), DEGREE, axis=0)
        + matmul(sender_rows, w_send)
        + matmul(edge_feats, w_edge)
        + b_edge
    )
    hidden = jax.nn.silu(pre_edge).astype(jnp.bfloat16)
    live = (
        (jnp.arange(DEGREE, dtype=jnp.int32)[None, :] < own_counts[:, None])
        .astype(jnp.float32)
        .reshape(-1, 1)
    )
    d_msg = (
        (edge_cot.astype(jnp.float32) + jnp.repeat(d_agg.astype(jnp.float32), DEGREE, axis=0))
        * live
    ).astype(jnp.bfloat16)
    d_pre = (matmul(d_msg, w_out.T) * slope(pre_edge)).astype(jnp.bfloat16)
    edge_grad = matmul(d_pre, w_edge.T).astype(jnp.bfloat16)
    to_recv = matmul(d_pre, w_recv.T).reshape(share, DEGREE, width).sum(axis=1)
    to_send = jax.ops.segment_sum(matmul(d_pre, w_send.T), senders, num_segments=nodes + 2 * halo, mode="promise_in_bounds"
    )
    local = to_send[:nodes]
    cot_lower = to_send[nodes : nodes + halo]
    cot_upper = to_send[nodes + halo :]
    back_upper = passed_along(cot_lower.astype(jnp.bfloat16), "sky", -1)
    back_lower = passed_along(cot_upper.astype(jnp.bfloat16), "sky", 1)
    local = local + spread(upper_pick, back_upper)
    local = local + spread(lower_pick, back_lower)
    recv_grad = jnp.einsum(
        "nf,nkg->fg", own, d_pre.reshape(share, DEGREE, width), preferred_element_type=jnp.float32
    )
    bias_terms = jnp.stack(
        [
            jnp.sum(d_pre.astype(jnp.float32), axis=0),
            jnp.sum(d_pre_node.astype(jnp.float32), axis=0),
        ]
    )
    terms = jnp.concatenate(
        [
            recv_grad,
            outer_sum(sender_rows, d_pre),
            outer_sum(edge_feats, d_pre),
            outer_sum(hidden, d_msg),
            outer_sum(own, d_pre_node),
            outer_sum(own_agg, d_pre_node),
            outer_sum(node_act, own_cot),
            bias_terms,
        ],
        axis=0,
    )
    used = terms.shape[0]
    chunk = -(-used // (groups * 8)) * 8
    terms = jnp.pad(terms, ((0, chunk * groups - used), (0, 0)))
    sky_bits = lax.axis_size("sky").bit_length() - 1
    early = min(EARLY_ROUNDS, sky_bits)
    for bit in range(early):
        got = exchanged(terms, "sky", bit)
        terms = terms + got
    mine = lax.dynamic_slice_in_dim(local, start, share, 0) + d_node + to_recv
    local = lax.dynamic_update_slice_in_dim(local, mine, start, 0)
    summed = halving_sum(local.reshape(groups, share, width), "edge", member, EDGE_ORDER, jnp.bfloat16)
    node_grad = doubling_gather(summed.astype(jnp.bfloat16), "edge", member, EDGE_ORDER)
    totals = halving_sum(terms.reshape(groups, chunk, width), "edge", member, EDGE_ORDER)
    for bit in range(early, sky_bits):
        totals = totals + exchanged(totals, "sky", bit)
    totals = doubling_gather(totals, "edge", member, EDGE_ORDER)[:used]
    scale = 1.0 / jnp.sqrt(jnp.float32(lax.axis_size("sky") * nodes * DEGREE))
    totals = totals * scale
    blocks = width
    edge_total = totals[: 4 * blocks].reshape(4, blocks, width)
    node_total = totals[4 * blocks : 7 * blocks].reshape(3, blocks, width)
    bias_total = totals[7 * blocks :]
    return (node_grad, edge_grad, edge_total, node_total, bias_total)


def solution(mesh):
    in_specs = (
        P("sky", None),
        P("sky", None),
        P("sky", None),
        P(("sky", "edge"), None),
        P(("sky", "edge"), None),
        P(("sky", "edge")),
        P("sky"),
        P("sky"),
        P("sky"),
        P(),
        P(),
        P(),
        P(),
        P(),
        P(),
        P(),
        P(),
        P(),
    )
    out_specs = (P("sky", None), P(("sky", "edge"), None), P(), P(), P())
    return jax.shard_map(layer, mesh=mesh, in_specs=in_specs, out_specs=out_specs, check_vma=False)
```

```python
import jax
import jax.numpy as jnp
from jax import lax
from jax.sharding import PartitionSpec as P


DEGREE = 16


def passed_along(array, axis, by):
    size = lax.axis_size(axis)
    return lax.ppermute(array, axis, [(i, (i + by) % size) for i in range(size)])


EDGE_ORDER = (1, 2, 0)
EARLY_ROUNDS = 3


def exchanged(array, axis, bit):
    size = lax.axis_size(axis)
    return lax.ppermute(array, axis, [(i, i ^ (1 << bit)) for i in range(size)])


def halving_sum(blocks, axis, me, order, wire=None):
    bits = len(order)
    rest = blocks.shape[1:]
    x = blocks.reshape((2,) * bits + rest)
    axes = list(range(bits - 1, -1, -1))
    for bit in order:
        at = axes.index(bit)
        keep = (me >> bit) & 1
        mine = lax.dynamic_index_in_dim(x, keep, axis=at, keepdims=False)
        other = lax.dynamic_index_in_dim(x, 1 - keep, axis=at, keepdims=False)
        if wire is None:
            x = mine + exchanged(other, axis, bit)
        else:
            x = mine + exchanged(other.astype(wire), axis, bit).astype(mine.dtype)
        axes.pop(at)
    return x


def doubling_gather(block, axis, me, order):
    axes = []
    for bit in reversed(order):
        got = exchanged(block, axis, bit)
        low = ((me >> bit) & 1) == 0
        block = jnp.where(low, jnp.stack([block, got]), jnp.stack([got, block]))
        axes.insert(0, bit)
    bits = len(order)
    block = jnp.transpose(block, [axes.index(b) for b in range(bits - 1, -1, -1)] + list(range(bits, block.ndim)))
    return block.reshape((-1,) + block.shape[bits + 1 :])


def picker(rows, size):
    return (rows[:, None] == lax.broadcasted_iota(jnp.int32, (1, size), 1)).astype(jnp.bfloat16)


def spread(pick, values):
    return lax.dot_general(
        pick, values, (((0,), (0,)), ((), ())), preferred_element_type=jnp.float32
    )


def slope(z):
    s = jax.nn.sigmoid(z)
    return s * (1.0 + z * (1.0 - s))


def matmul(a, b):
    return jnp.dot(a, b, preferred_element_type=jnp.float32)


def outer_sum(a, b):
    return jnp.einsum("ef,eg->fg", a, b, preferred_element_type=jnp.float32)


def layer(
    node_feats,
    saved_agg,
    node_cot,
    edge_feats,
    edge_cot,
    senders,
    counts,
    send_lower,
    send_upper,
    w_recv,
    w_send,
    w_edge,
    w_out,
    b_edge,
    v_self,
    v_agg,
    v_out,
    b_node,
):
    nodes = node_feats.shape[0]
    width = node_feats.shape[1]
    halo = send_lower.shape[0]
    groups = lax.axis_size("edge")
    member = lax.axis_index("edge")
    share = nodes // groups
    start = member * share
    upper_pick = picker(send_upper, nodes)
    lower_pick = picker(send_lower, nodes)
    upper_rows = matmul(upper_pick, node_feats).astype(jnp.bfloat16)
    lower_rows = matmul(lower_pick, node_feats).astype(jnp.bfloat16)
    from_lower = passed_along(upper_rows, "sky", 1)
    from_upper = passed_along(lower_rows, "sky", -1)
    all_rows = jnp.concatenate([node_feats, from_lower, from_upper], axis=0)
    own = lax.dynamic_slice_in_dim(node_feats, start, share, 0)
    own_agg = lax.dynamic_slice_in_dim(saved_agg, start, share, 0)
    own_cot = lax.dynamic_slice_in_dim(node_cot, start, share, 0)
    own_counts = lax.dynamic_slice_in_dim(counts, start, share, 0)
    pre_node = matmul(own, v_self) + matmul(own_agg, v_agg) + b_node
    node_act = jax.nn.silu(pre_node).astype(jnp.bfloat16)
    d_pre_node = (matmul(own_cot, v_out.T) * slope(pre_node)).astype(jnp.bfloat16)
    d_agg = matmul(d_pre_node, v_agg.T).astype(jnp.bfloat16)
    d_node = own_cot.astype(jnp.float32) + matmul(d_pre_node, v_self.T)
    sender_rows = all_rows.at[senders].get(mode="promise_in_bounds")
    pre_edge = (
        jnp.repeat(matmul(own, w_recv), DEGREE, axis=0)
        + matmul(sender_rows, w_send)
        + matmul(edge_feats, w_edge)
        + b_edge
    )
    hidden = jax.nn.silu(pre_edge).astype(jnp.bfloat16)
    live = (
        (jnp.arange(DEGREE, dtype=jnp.int32)[None, :] < own_counts[:, None])
        .astype(jnp.float32)
        .reshape(-1, 1)
    )
    d_msg = (
        (edge_cot.astype(jnp.float32) + jnp.repeat(d_agg.astype(jnp.float32), DEGREE, axis=0))
        * live
    ).astype(jnp.bfloat16)
    d_pre = (matmul(d_msg, w_out.T) * slope(pre_edge)).astype(jnp.bfloat16)
    edge_grad = matmul(d_pre, w_edge.T).astype(jnp.bfloat16)
    to_recv = matmul(d_pre, w_recv.T).reshape(share, DEGREE, width).sum(axis=1)
    to_send = jax.ops.segment_sum(matmul(d_pre, w_send.T), senders, num_segments=nodes + 2 * halo, mode="promise_in_bounds"
    )
    local = to_send[:nodes]
    cot_lower = to_send[nodes : nodes + halo]
    cot_upper = to_send[nodes + halo :]
    back_upper = passed_along(cot_lower.astype(jnp.bfloat16), "sky", -1)
    back_lower = passed_along(cot_upper.astype(jnp.bfloat16), "sky", 1)
    local = local + spread(upper_pick, back_upper)
    local = local + spread(lower_pick, back_lower)
    recv_grad = jnp.einsum(
        "nf,nkg->fg", own, d_pre.reshape(share, DEGREE, width), preferred_element_type=jnp.float32
    )
    bias_terms = jnp.stack(
        [
            jnp.sum(d_pre.astype(jnp.float32), axis=0),
            jnp.sum(d_pre_node.astype(jnp.float32), axis=0),
        ]
    )
    terms = jnp.concatenate(
        [
            recv_grad,
            outer_sum(sender_rows, d_pre),
            outer_sum(edge_feats, d_pre),
            outer_sum(hidden, d_msg),
            outer_sum(own, d_pre_node),
            outer_sum(own_agg, d_pre_node),
            outer_sum(node_act, own_cot),
            bias_terms,
        ],
        axis=0,
    )
    used = terms.shape[0]
    chunk = -(-used // (groups * 8)) * 8
    terms = jnp.pad(terms, ((0, chunk * groups - used), (0, 0)))
    sky_bits = lax.axis_size("sky").bit_length() - 1
    sky_order = list(range(1, sky_bits)) + [0]
    early = min(EARLY_ROUNDS, sky_bits)
    for bit in sky_order[:early]:
        got = exchanged(terms, "sky", bit)
        terms = terms + got
    mine = lax.dynamic_slice_in_dim(local, start, share, 0) + d_node + to_recv
    local = lax.dynamic_update_slice_in_dim(local, mine, start, 0)
    summed = halving_sum(local.reshape(groups, share, width), "edge", member, EDGE_ORDER, jnp.bfloat16)
    node_grad = doubling_gather(summed.astype(jnp.bfloat16), "edge", member, EDGE_ORDER)
    totals = halving_sum(terms.reshape(groups, chunk, width), "edge", member, EDGE_ORDER)
    for bit in sky_order[early:]:
        totals = totals + exchanged(totals, "sky", bit)
    totals = doubling_gather(totals, "edge", member, EDGE_ORDER)[:used]
    scale = 1.0 / jnp.sqrt(jnp.float32(lax.axis_size("sky") * nodes * DEGREE))
    totals = totals * scale
    blocks = width
    edge_total = totals[: 4 * blocks].reshape(4, blocks, width)
    node_total = totals[4 * blocks : 7 * blocks].reshape(3, blocks, width)
    bias_total = totals[7 * blocks :]
    return (node_grad, edge_grad, edge_total, node_total, bias_total)


def solution(mesh):
    in_specs = (
        P("sky", None),
        P("sky", None),
        P("sky", None),
        P(("sky", "edge"), None),
        P(("sky", "edge"), None),
        P(("sky", "edge")),
        P("sky"),
        P("sky"),
        P("sky"),
        P(),
        P(),
        P(),
        P(),
        P(),
        P(),
        P(),
        P(),
        P(),
    )
    out_specs = (P("sky", None), P(("sky", "edge"), None), P(), P(), P())
    return jax.shard_map(layer, mesh=mesh, in_specs=in_specs, out_specs=out_specs, check_vma=False)
```

```python
import jax
import jax.numpy as jnp
from jax import lax
from jax.sharding import PartitionSpec as P


DEGREE = 16


def passed_along(array, axis, by):
    size = lax.axis_size(axis)
    return lax.ppermute(array, axis, [(i, (i + by) % size) for i in range(size)])


EDGE_ORDER = (1, 2, 0)
EARLY_ROUNDS = 5
SCATTER_PIECES = 4


def exchanged(array, axis, bit):
    size = lax.axis_size(axis)
    return lax.ppermute(array, axis, [(i, i ^ (1 << bit)) for i in range(size)])


def halving_sum(blocks, axis, me, order, wire=None):
    bits = len(order)
    rest = blocks.shape[1:]
    x = blocks.reshape((2,) * bits + rest)
    axes = list(range(bits - 1, -1, -1))
    for bit in order:
        at = axes.index(bit)
        keep = (me >> bit) & 1
        mine = lax.dynamic_index_in_dim(x, keep, axis=at, keepdims=False)
        other = lax.dynamic_index_in_dim(x, 1 - keep, axis=at, keepdims=False)
        if wire is None:
            x = mine + exchanged(other, axis, bit)
        else:
            x = mine + exchanged(other.astype(wire), axis, bit).astype(mine.dtype)
        axes.pop(at)
    return x


def doubling_gather(block, axis, me, order):
    axes = []
    for bit in reversed(order):
        got = exchanged(block, axis, bit)
        low = ((me >> bit) & 1) == 0
        block = jnp.where(low, jnp.stack([block, got]), jnp.stack([got, block]))
        axes.insert(0, bit)
    bits = len(order)
    block = jnp.transpose(block, [axes.index(b) for b in range(bits - 1, -1, -1)] + list(range(bits, block.ndim)))
    return block.reshape((-1,) + block.shape[bits + 1 :])


def picker(rows, size):
    return (rows[:, None] == lax.broadcasted_iota(jnp.int32, (1, size), 1)).astype(jnp.bfloat16)


def spread(pick, values):
    return lax.dot_general(
        pick, values, (((0,), (0,)), ((), ())), preferred_element_type=jnp.float32
    )


def slope(z):
    s = jax.nn.sigmoid(z)
    return s * (1.0 + z * (1.0 - s))


def matmul(a, b):
    return jnp.dot(a, b, preferred_element_type=jnp.float32)


def outer_sum(a, b):
    return jnp.einsum("ef,eg->fg", a, b, preferred_element_type=jnp.float32)


def layer(
    node_feats,
    saved_agg,
    node_cot,
    edge_feats,
    edge_cot,
    senders,
    counts,
    send_lower,
    send_upper,
    w_recv,
    w_send,
    w_edge,
    w_out,
    b_edge,
    v_self,
    v_agg,
    v_out,
    b_node,
):
    nodes = node_feats.shape[0]
    width = node_feats.shape[1]
    halo = send_lower.shape[0]
    groups = lax.axis_size("edge")
    member = lax.axis_index("edge")
    share = nodes // groups
    start = member * share
    upper_pick = picker(send_upper, nodes)
    lower_pick = picker(send_lower, nodes)
    upper_rows = matmul(upper_pick, node_feats).astype(jnp.bfloat16)
    lower_rows = matmul(lower_pick, node_feats).astype(jnp.bfloat16)
    from_lower = passed_along(upper_rows, "sky", 1)
    from_upper = passed_along(lower_rows, "sky", -1)
    all_rows = jnp.concatenate([node_feats, from_lower, from_upper], axis=0)
    own = lax.dynamic_slice_in_dim(node_feats, start, share, 0)
    own_agg = lax.dynamic_slice_in_dim(saved_agg, start, share, 0)
    own_cot = lax.dynamic_slice_in_dim(node_cot, start, share, 0)
    own_counts = lax.dynamic_slice_in_dim(counts, start, share, 0)
    pre_node = matmul(own, v_self) + matmul(own_agg, v_agg) + b_node
    node_act = jax.nn.silu(pre_node).astype(jnp.bfloat16)
    d_pre_node = (matmul(own_cot, v_out.T) * slope(pre_node)).astype(jnp.bfloat16)
    d_agg = matmul(d_pre_node, v_agg.T).astype(jnp.bfloat16)
    d_node = own_cot.astype(jnp.float32) + matmul(d_pre_node, v_self.T)
    sender_rows = all_rows.at[senders].get(mode="promise_in_bounds")
    pre_edge = (
        jnp.repeat(matmul(own, w_recv), DEGREE, axis=0)
        + matmul(sender_rows, w_send)
        + matmul(edge_feats, w_edge)
        + b_edge
    )
    hidden = jax.nn.silu(pre_edge).astype(jnp.bfloat16)
    live = (
        (jnp.arange(DEGREE, dtype=jnp.int32)[None, :] < own_counts[:, None])
        .astype(jnp.float32)
        .reshape(-1, 1)
    )
    d_msg = (
        (edge_cot.astype(jnp.float32) + jnp.repeat(d_agg.astype(jnp.float32), DEGREE, axis=0))
        * live
    ).astype(jnp.bfloat16)
    d_pre = (matmul(d_msg, w_out.T) * slope(pre_edge)).astype(jnp.bfloat16)
    edge_grad = matmul(d_pre, w_edge.T).astype(jnp.bfloat16)
    to_recv = matmul(d_pre, w_recv.T).reshape(share, DEGREE, width).sum(axis=1)
    messages = matmul(d_pre, w_send.T)
    pieces = SCATTER_PIECES
    step_rows = messages.shape[0] // pieces
    to_send = jnp.zeros((nodes + 2 * halo, width), jnp.float32)
    for piece in range(pieces):
        rows = slice(piece * step_rows, (piece + 1) * step_rows)
        to_send = to_send.at[senders[rows]].add(messages[rows], mode="promise_in_bounds")
    local = to_send[:nodes]
    cot_lower = to_send[nodes : nodes + halo]
    cot_upper = to_send[nodes + halo :]
    back_upper = passed_along(cot_lower.astype(jnp.bfloat16), "sky", -1)
    back_lower = passed_along(cot_upper.astype(jnp.bfloat16), "sky", 1)
    local = local + spread(upper_pick, back_upper)
    local = local + spread(lower_pick, back_lower)
    recv_grad = jnp.einsum(
        "nf,nkg->fg", own, d_pre.reshape(share, DEGREE, width), preferred_element_type=jnp.float32
    )
    bias_terms = jnp.stack(
        [
            jnp.sum(d_pre.astype(jnp.float32), axis=0),
            jnp.sum(d_pre_node.astype(jnp.float32), axis=0),
        ]
    )
    terms = jnp.concatenate(
        [
            recv_grad,
            outer_sum(sender_rows, d_pre),
            outer_sum(edge_feats, d_pre),
            outer_sum(hidden, d_msg),
            outer_sum(own, d_pre_node),
            outer_sum(own_agg, d_pre_node),
            outer_sum(node_act, own_cot),
            bias_terms,
        ],
        axis=0,
    )
    used = terms.shape[0]
    chunk = -(-used // (groups * 8)) * 8
    terms = jnp.pad(terms, ((0, chunk * groups - used), (0, 0)))
    sky_bits = lax.axis_size("sky").bit_length() - 1
    early = min(EARLY_ROUNDS, sky_bits)
    for bit in range(early):
        got = exchanged(terms, "sky", bit)
        terms = terms + got
    mine = lax.dynamic_slice_in_dim(local, start, share, 0) + d_node + to_recv
    local = lax.dynamic_update_slice_in_dim(local, mine, start, 0)
    summed = halving_sum(local.reshape(groups, share, width), "edge", member, EDGE_ORDER, jnp.bfloat16)
    node_grad = doubling_gather(summed.astype(jnp.bfloat16), "edge", member, EDGE_ORDER)
    totals = halving_sum(terms.reshape(groups, chunk, width), "edge", member, EDGE_ORDER)
    for bit in range(early, sky_bits):
        totals = totals + exchanged(totals, "sky", bit)
    totals = doubling_gather(totals, "edge", member, EDGE_ORDER)[:used]
    scale = 1.0 / jnp.sqrt(jnp.float32(lax.axis_size("sky") * nodes * DEGREE))
    totals = totals * scale
    blocks = width
    edge_total = totals[: 4 * blocks].reshape(4, blocks, width)
    node_total = totals[4 * blocks : 7 * blocks].reshape(3, blocks, width)
    bias_total = totals[7 * blocks :]
    return (node_grad, edge_grad, edge_total, node_total, bias_total)


def solution(mesh):
    in_specs = (
        P("sky", None),
        P("sky", None),
        P("sky", None),
        P(("sky", "edge"), None),
        P(("sky", "edge"), None),
        P(("sky", "edge")),
        P("sky"),
        P("sky"),
        P("sky"),
        P(),
        P(),
        P(),
        P(),
        P(),
        P(),
        P(),
        P(),
        P(),
    )
    out_specs = (P("sky", None), P(("sky", "edge"), None), P(), P(), P())
    return jax.shard_map(layer, mesh=mesh, in_specs=in_specs, out_specs=out_specs, check_vma=False)
```

```python
import jax
import jax.numpy as jnp
from jax import lax
from jax.sharding import PartitionSpec as P


DEGREE = 16


def passed_along(array, axis, by):
    size = lax.axis_size(axis)
    return lax.ppermute(array, axis, [(i, (i + by) % size) for i in range(size)])


EDGE_ORDER = (1, 2, 0)
EARLY_ROUNDS = 5
SCATTER_PIECES = 4


def exchanged(array, axis, bit):
    size = lax.axis_size(axis)
    return lax.ppermute(array, axis, [(i, i ^ (1 << bit)) for i in range(size)])


def halving_sum(blocks, axis, me, order, wire=None):
    bits = len(order)
    rest = blocks.shape[1:]
    x = blocks.reshape((2,) * bits + rest)
    axes = list(range(bits - 1, -1, -1))
    for bit in order:
        at = axes.index(bit)
        keep = (me >> bit) & 1
        mine = lax.dynamic_index_in_dim(x, keep, axis=at, keepdims=False)
        other = lax.dynamic_index_in_dim(x, 1 - keep, axis=at, keepdims=False)
        if wire is None:
            x = mine + exchanged(other, axis, bit)
        else:
            x = mine + exchanged(other.astype(wire), axis, bit).astype(mine.dtype)
        axes.pop(at)
    return x


def doubling_gather(block, axis, me, order):
    axes = []
    for bit in reversed(order):
        got = exchanged(block, axis, bit)
        low = ((me >> bit) & 1) == 0
        block = jnp.where(low, jnp.stack([block, got]), jnp.stack([got, block]))
        axes.insert(0, bit)
    bits = len(order)
    block = jnp.transpose(block, [axes.index(b) for b in range(bits - 1, -1, -1)] + list(range(bits, block.ndim)))
    return block.reshape((-1,) + block.shape[bits + 1 :])


def picker(rows, size):
    return (rows[:, None] == lax.broadcasted_iota(jnp.int32, (1, size), 1)).astype(jnp.bfloat16)


def spread(rows, size, values):
    pick = (lax.broadcasted_iota(jnp.int32, (size, 1), 0) == rows[None, :]).astype(jnp.bfloat16)
    return matmul(pick, values)


def slope(z):
    s = jax.nn.sigmoid(z)
    return s * (1.0 + z * (1.0 - s))


def matmul(a, b):
    return jnp.dot(a, b, preferred_element_type=jnp.float32)


def outer_sum(a, b):
    return jnp.einsum("ef,eg->fg", a, b, preferred_element_type=jnp.float32)


def layer(
    node_feats,
    saved_agg,
    node_cot,
    edge_feats,
    edge_cot,
    senders,
    counts,
    send_lower,
    send_upper,
    w_recv,
    w_send,
    w_edge,
    w_out,
    b_edge,
    v_self,
    v_agg,
    v_out,
    b_node,
):
    nodes = node_feats.shape[0]
    width = node_feats.shape[1]
    halo = send_lower.shape[0]
    groups = lax.axis_size("edge")
    member = lax.axis_index("edge")
    share = nodes // groups
    start = member * share
    both_lists = jnp.concatenate([send_upper, send_lower])
    both_rows = matmul(picker(both_lists, nodes), node_feats).astype(jnp.bfloat16)
    upper_rows = both_rows[:halo]
    lower_rows = both_rows[halo:]
    from_lower = passed_along(upper_rows, "sky", 1)
    from_upper = passed_along(lower_rows, "sky", -1)
    all_rows = jnp.concatenate([node_feats, from_lower, from_upper], axis=0)
    own = lax.dynamic_slice_in_dim(node_feats, start, share, 0)
    own_agg = lax.dynamic_slice_in_dim(saved_agg, start, share, 0)
    own_cot = lax.dynamic_slice_in_dim(node_cot, start, share, 0)
    own_counts = lax.dynamic_slice_in_dim(counts, start, share, 0)
    pre_node = matmul(own, v_self) + matmul(own_agg, v_agg) + b_node
    node_act = jax.nn.silu(pre_node).astype(jnp.bfloat16)
    d_pre_node = (matmul(own_cot, v_out.T) * slope(pre_node)).astype(jnp.bfloat16)
    d_agg = matmul(d_pre_node, v_agg.T).astype(jnp.bfloat16)
    d_node = own_cot.astype(jnp.float32) + matmul(d_pre_node, v_self.T)
    sender_rows = all_rows.at[senders].get(mode="promise_in_bounds")
    pre_edge = (
        jnp.repeat(matmul(own, w_recv), DEGREE, axis=0)
        + matmul(sender_rows, w_send)
        + matmul(edge_feats, w_edge)
        + b_edge
    )
    hidden = jax.nn.silu(pre_edge).astype(jnp.bfloat16)
    live = (
        (jnp.arange(DEGREE, dtype=jnp.int32)[None, :] < own_counts[:, None])
        .astype(jnp.float32)
        .reshape(-1, 1)
    )
    d_msg = (
        (edge_cot.astype(jnp.float32) + jnp.repeat(d_agg.astype(jnp.float32), DEGREE, axis=0))
        * live
    ).astype(jnp.bfloat16)
    d_pre = (matmul(d_msg, w_out.T) * slope(pre_edge)).astype(jnp.bfloat16)
    edge_grad = matmul(d_pre, w_edge.T).astype(jnp.bfloat16)
    to_recv = matmul(d_pre, w_recv.T).reshape(share, DEGREE, width).sum(axis=1)
    messages = matmul(d_pre, w_send.T)
    pieces = SCATTER_PIECES
    step_rows = messages.shape[0] // pieces
    to_send = jnp.zeros((nodes + 2 * halo, width), jnp.float32)
    for piece in range(pieces):
        rows = slice(piece * step_rows, (piece + 1) * step_rows)
        to_send = to_send.at[senders[rows]].add(messages[rows], mode="promise_in_bounds")
    local = to_send[:nodes]
    cot_lower = to_send[nodes : nodes + halo]
    cot_upper = to_send[nodes + halo :]
    back_upper = passed_along(cot_lower.astype(jnp.bfloat16), "sky", -1)
    back_lower = passed_along(cot_upper.astype(jnp.bfloat16), "sky", 1)
    local = local + spread(both_lists, nodes, jnp.concatenate([back_upper, back_lower]))
    recv_grad = jnp.einsum(
        "nf,nkg->fg", own, d_pre.reshape(share, DEGREE, width), preferred_element_type=jnp.float32
    )
    bias_terms = jnp.stack(
        [
            jnp.sum(d_pre.astype(jnp.float32), axis=0),
            jnp.sum(d_pre_node.astype(jnp.float32), axis=0),
        ]
    )
    terms = jnp.concatenate(
        [
            recv_grad,
            outer_sum(sender_rows, d_pre),
            outer_sum(edge_feats, d_pre),
            outer_sum(hidden, d_msg),
            outer_sum(own, d_pre_node),
            outer_sum(own_agg, d_pre_node),
            outer_sum(node_act, own_cot),
            bias_terms,
        ],
        axis=0,
    )
    used = terms.shape[0]
    chunk = -(-used // (groups * 8)) * 8
    terms = jnp.pad(terms, ((0, chunk * groups - used), (0, 0)))
    sky_bits = lax.axis_size("sky").bit_length() - 1
    early = min(EARLY_ROUNDS, sky_bits)
    for bit in range(early):
        got = exchanged(terms, "sky", bit)
        terms = terms + got
    mine = lax.dynamic_slice_in_dim(local, start, share, 0) + d_node + to_recv
    local = lax.dynamic_update_slice_in_dim(local, mine, start, 0)
    summed = halving_sum(local.reshape(groups, share, width), "edge", member, EDGE_ORDER, jnp.bfloat16)
    node_grad = doubling_gather(summed.astype(jnp.bfloat16), "edge", member, EDGE_ORDER)
    totals = halving_sum(terms.reshape(groups, chunk, width), "edge", member, EDGE_ORDER)
    for bit in range(early, sky_bits):
        totals = totals + exchanged(totals, "sky", bit)
    totals = doubling_gather(totals, "edge", member, EDGE_ORDER)[:used]
    scale = 1.0 / jnp.sqrt(jnp.float32(lax.axis_size("sky") * nodes * DEGREE))
    totals = totals * scale
    blocks = width
    edge_total = totals[: 4 * blocks].reshape(4, blocks, width)
    node_total = totals[4 * blocks : 7 * blocks].reshape(3, blocks, width)
    bias_total = totals[7 * blocks :]
    return (node_grad, edge_grad, edge_total, node_total, bias_total)


def solution(mesh):
    in_specs = (
        P("sky", None),
        P("sky", None),
        P("sky", None),
        P(("sky", "edge"), None),
        P(("sky", "edge"), None),
        P(("sky", "edge")),
        P("sky"),
        P("sky"),
        P("sky"),
        P(),
        P(),
        P(),
        P(),
        P(),
        P(),
        P(),
        P(),
        P(),
    )
    out_specs = (P("sky", None), P(("sky", "edge"), None), P(), P(), P())
    return jax.shard_map(layer, mesh=mesh, in_specs=in_specs, out_specs=out_specs, check_vma=False)
```

```python
import jax
import jax.numpy as jnp
from jax import lax
from jax.sharding import PartitionSpec as P


DEGREE = 16


def passed_along(array, axis, by):
    size = lax.axis_size(axis)
    return lax.ppermute(array, axis, [(i, (i + by) % size) for i in range(size)])


EDGE_ORDER = (1, 0, 2)
EARLY_ROUNDS = 5
SCATTER_PIECES = 4


def exchanged(array, axis, bit):
    size = lax.axis_size(axis)
    return lax.ppermute(array, axis, [(i, i ^ (1 << bit)) for i in range(size)])


def halving_sum(blocks, axis, me, order, wire=None):
    bits = len(order)
    rest = blocks.shape[1:]
    x = blocks.reshape((2,) * bits + rest)
    axes = list(range(bits - 1, -1, -1))
    for bit in order:
        at = axes.index(bit)
        keep = (me >> bit) & 1
        mine = lax.dynamic_index_in_dim(x, keep, axis=at, keepdims=False)
        other = lax.dynamic_index_in_dim(x, 1 - keep, axis=at, keepdims=False)
        if wire is None:
            x = mine + exchanged(other, axis, bit)
        else:
            x = mine + exchanged(other.astype(wire), axis, bit).astype(mine.dtype)
        axes.pop(at)
    return x


def doubling_gather(block, axis, me, order):
    axes = []
    for bit in reversed(order):
        got = exchanged(block, axis, bit)
        low = ((me >> bit) & 1) == 0
        block = jnp.where(low, jnp.stack([block, got]), jnp.stack([got, block]))
        axes.insert(0, bit)
    bits = len(order)
    block = jnp.transpose(block, [axes.index(b) for b in range(bits - 1, -1, -1)] + list(range(bits, block.ndim)))
    return block.reshape((-1,) + block.shape[bits + 1 :])


def picker(rows, size):
    return (rows[:, None] == lax.broadcasted_iota(jnp.int32, (1, size), 1)).astype(jnp.bfloat16)


def spread(rows, size, values):
    pick = (lax.broadcasted_iota(jnp.int32, (size, 1), 0) == rows[None, :]).astype(jnp.bfloat16)
    return matmul(pick, values)


def slope(z):
    s = jax.nn.sigmoid(z)
    return s * (1.0 + z * (1.0 - s))


def matmul(a, b):
    return jnp.dot(a, b, preferred_element_type=jnp.float32)


def outer_sum(a, b):
    return jnp.einsum("ef,eg->fg", a, b, preferred_element_type=jnp.float32)


def layer(
    node_feats,
    saved_agg,
    node_cot,
    edge_feats,
    edge_cot,
    senders,
    counts,
    send_lower,
    send_upper,
    w_recv,
    w_send,
    w_edge,
    w_out,
    b_edge,
    v_self,
    v_agg,
    v_out,
    b_node,
):
    nodes = node_feats.shape[0]
    width = node_feats.shape[1]
    halo = send_lower.shape[0]
    groups = lax.axis_size("edge")
    member = lax.axis_index("edge")
    share = nodes // groups
    start = member * share
    upper_pick = picker(send_upper, nodes)
    lower_pick = picker(send_lower, nodes)
    upper_rows = matmul(upper_pick, node_feats).astype(jnp.bfloat16)
    lower_rows = matmul(lower_pick, node_feats).astype(jnp.bfloat16)
    from_lower = passed_along(upper_rows, "sky", 1)
    from_upper = passed_along(lower_rows, "sky", -1)
    all_rows = jnp.concatenate([node_feats, from_lower, from_upper], axis=0)
    own = lax.dynamic_slice_in_dim(node_feats, start, share, 0)
    own_agg = lax.dynamic_slice_in_dim(saved_agg, start, share, 0)
    own_cot = lax.dynamic_slice_in_dim(node_cot, start, share, 0)
    own_counts = lax.dynamic_slice_in_dim(counts, start, share, 0)
    pre_node = matmul(own, v_self) + matmul(own_agg, v_agg) + b_node
    node_act = jax.nn.silu(pre_node).astype(jnp.bfloat16)
    d_pre_node = (matmul(own_cot, v_out.T) * slope(pre_node)).astype(jnp.bfloat16)
    d_agg = matmul(d_pre_node, v_agg.T).astype(jnp.bfloat16)
    d_node = own_cot.astype(jnp.float32) + matmul(d_pre_node, v_self.T)
    sender_rows = all_rows.at[senders].get(mode="promise_in_bounds")
    pre_edge = (
        jnp.repeat(matmul(own, w_recv), DEGREE, axis=0)
        + matmul(sender_rows, w_send)
        + matmul(edge_feats, w_edge)
        + b_edge
    )
    hidden = jax.nn.silu(pre_edge).astype(jnp.bfloat16)
    live = (
        (jnp.arange(DEGREE, dtype=jnp.int32)[None, :] < own_counts[:, None])
        .astype(jnp.float32)
        .reshape(-1, 1)
    )
    d_msg = (
        (edge_cot.astype(jnp.float32) + jnp.repeat(d_agg.astype(jnp.float32), DEGREE, axis=0))
        * live
    ).astype(jnp.bfloat16)
    d_pre = (matmul(d_msg, w_out.T) * slope(pre_edge)).astype(jnp.bfloat16)
    edge_grad = matmul(d_pre, w_edge.T).astype(jnp.bfloat16)
    to_recv = matmul(d_pre, w_recv.T).reshape(share, DEGREE, width).sum(axis=1)
    messages = matmul(d_pre, w_send.T)
    pieces = SCATTER_PIECES
    step_rows = messages.shape[0] // pieces
    to_send = jnp.zeros((nodes + 2 * halo, width), jnp.float32)
    for piece in range(pieces):
        rows = slice(piece * step_rows, (piece + 1) * step_rows)
        to_send = to_send.at[senders[rows]].add(messages[rows], mode="promise_in_bounds")
    local = to_send[:nodes]
    cot_lower = to_send[nodes : nodes + halo]
    cot_upper = to_send[nodes + halo :]
    back_upper = passed_along(cot_lower.astype(jnp.bfloat16), "sky", -1)
    back_lower = passed_along(cot_upper.astype(jnp.bfloat16), "sky", 1)
    local = local + spread(send_upper, nodes, back_upper)
    local = local + spread(send_lower, nodes, back_lower)
    recv_grad = jnp.einsum(
        "nf,nkg->fg", own, d_pre.reshape(share, DEGREE, width), preferred_element_type=jnp.float32
    )
    bias_terms = jnp.stack(
        [
            jnp.sum(d_pre.astype(jnp.float32), axis=0),
            jnp.sum(d_pre_node.astype(jnp.float32), axis=0),
        ]
    )
    terms = jnp.concatenate(
        [
            recv_grad,
            outer_sum(sender_rows, d_pre),
            outer_sum(edge_feats, d_pre),
            outer_sum(hidden, d_msg),
            outer_sum(own, d_pre_node),
            outer_sum(own_agg, d_pre_node),
            outer_sum(node_act, own_cot),
            bias_terms,
        ],
        axis=0,
    )
    used = terms.shape[0]
    chunk = -(-used // (groups * 8)) * 8
    terms = jnp.pad(terms, ((0, chunk * groups - used), (0, 0)))
    sky_bits = lax.axis_size("sky").bit_length() - 1
    early = min(EARLY_ROUNDS, sky_bits)
    for bit in range(early):
        got = exchanged(terms, "sky", bit)
        terms = terms + got
    mine = lax.dynamic_slice_in_dim(local, start, share, 0) + d_node + to_recv
    local = lax.dynamic_update_slice_in_dim(local, mine, start, 0)
    summed = halving_sum(local.reshape(groups, share, width), "edge", member, EDGE_ORDER, jnp.bfloat16)
    node_grad = doubling_gather(summed.astype(jnp.bfloat16), "edge", member, EDGE_ORDER)
    totals = halving_sum(terms.reshape(groups, chunk, width), "edge", member, EDGE_ORDER)
    for bit in range(early, sky_bits):
        totals = totals + exchanged(totals, "sky", bit)
    totals = doubling_gather(totals, "edge", member, EDGE_ORDER)[:used]
    scale = 1.0 / jnp.sqrt(jnp.float32(lax.axis_size("sky") * nodes * DEGREE))
    totals = totals * scale
    blocks = width
    edge_total = totals[: 4 * blocks].reshape(4, blocks, width)
    node_total = totals[4 * blocks : 7 * blocks].reshape(3, blocks, width)
    bias_total = totals[7 * blocks :]
    return (node_grad, edge_grad, edge_total, node_total, bias_total)


def solution(mesh):
    in_specs = (
        P("sky", None),
        P("sky", None),
        P("sky", None),
        P(("sky", "edge"), None),
        P(("sky", "edge"), None),
        P(("sky", "edge")),
        P("sky"),
        P("sky"),
        P("sky"),
        P(),
        P(),
        P(),
        P(),
        P(),
        P(),
        P(),
        P(),
        P(),
    )
    out_specs = (P("sky", None), P(("sky", "edge"), None), P(), P(), P())
    return jax.shard_map(layer, mesh=mesh, in_specs=in_specs, out_specs=out_specs, check_vma=False)
```
